512 devices in a mesh: chan: 32 (over z_lo, y, core), day: 16 (over x, z_hi).
Axes of the slice: x: 4, y: 4, z: 16 (z_hi: 4, z_lo: 4; z = z_hi * 4 + z_lo), core: 2. Of those that a mesh axis runs over, the one named last changes fastest.
Arguments:
- records: bfloat16 [16, 2048, 4096], P('day', 'chan'), may hold values from -50 to 50
- filter_taps: bfloat16 [64], replicated, may hold values from -0.75 to 0.75
- window_offsets: int32 [16, 2], P('day'), may hold values from 0 to 3009, as said below
- pair_masks: int32 [3], replicated, may hold values from 1 to 31, as said below
Outputs:
- stacks: float32 [3, 65, 131072], P(None, None, ('chan', 'day'))
The draws below stay inside these ranges and needn't reach their ends.
Inputs may be any that keep to these rules, and one draw needn't show every extreme that they name: `window_offsets`: in each day group one window ends at the record's last sample. `pair_masks`: the masks are distinct; 1 and 31 are among them.
All inputs are finite; a program needn't handle non-finite values.
Results may differ from the reference program's by a relative error of at most 0.0029.
Values may be sent and summed in bfloat16 or wider, within the bound.
A program may use at most 64 MiB of HBM per device.

```python
import jax
import jax.numpy as jnp
from jax import lax

C_BLK = 64
L = 1024
TAPS = 64
MAXLAG = 32
ROUNDS = 3
WIN = 2
LAGS = 65
REC = 4096
MAXOFF = 3009
CHANNELS = 2048
DAYS = 16


def draw_records(key, part):
    first_key, second_key = jax.random.split(jax.random.fold_in(key, 11))
    shape = (DAYS, CHANNELS, REC)
    base = jnp.clip(jax.random.normal(first_key, shape, jnp.float32), -5.0, 5.0)
    spread = jnp.log(10.0)
    scales = jnp.exp(jax.random.uniform(second_key, (DAYS, CHANNELS, 1), jnp.float32) * spread)
    return (base * scales).astype(jnp.bfloat16)


def draw_window_offsets(key, part):
    first_key, second_key = jax.random.split(jax.random.fold_in(key, 23))
    values = jax.random.randint(first_key, (DAYS, WIN), 0, MAXOFF + 1, jnp.int32)
    places = jax.random.randint(second_key, (DAYS, 1), 0, WIN, jnp.int32)
    columns = jnp.arange(WIN, dtype=jnp.int32)[None, :]
    values = jnp.where(columns == places, MAXOFF, values)
    return values.astype(jnp.int32)


def draw_pair_masks(key, part):
    first_key, second_key = jax.random.split(jax.random.fold_in(key, 37))
    blocks_count = CHANNELS // C_BLK
    middle = jax.random.permutation(first_key, jnp.arange(2, blocks_count - 1, dtype=jnp.int32))[:ROUNDS - 2]
    chosen = jnp.concatenate([jnp.array([1, blocks_count - 1], jnp.int32), middle])
    return jax.random.permutation(second_key, chosen).astype(jnp.int32)


def scatter_about(own_key, shape, deviation, limit, kind=jnp.bfloat16):
    return jnp.clip(deviation * jax.random.normal(own_key, shape, jnp.float32), -limit, limit).astype(kind)


def setup_inputs(seed: int = 0) -> dict:
    keys = jax.random.split(jax.random.key(seed), 5)
    return {
        "records": draw_records(jax.random.fold_in(keys[4], 71), 0),
        "filter_taps": scatter_about(keys[1], (TAPS,), TAPS ** -0.5, 0.75),
        "window_offsets": draw_window_offsets(jax.random.fold_in(keys[4], 71), 0),
        "pair_masks": draw_pair_masks(jax.random.fold_in(keys[4], 71), 0),
    }


def whiten(segments, filter_taps):
    tap_count = filter_taps.shape[0]
    width = segments.shape[-1] - tap_count + 1
    taps_wide = filter_taps.astype(jnp.float32)
    total = jnp.zeros(segments.shape[:-1] + (width,), jnp.float32)
    for tap_index in range(tap_count):
        total = total + taps_wide[tap_index] * segments[..., tap_index:tap_index + width].astype(jnp.float32)
    power = lax.optimization_barrier(jnp.mean(total * total, axis=-1, keepdims=True))
    return (total * lax.rsqrt(power + 1e-06)).astype(jnp.bfloat16)

def reference(records, filter_taps, window_offsets, pair_masks):
    seg_len = L + TAPS - 1
    blocks_count = CHANNELS // C_BLK

    def cut_day(record, offsets_day):

        def cut_window(start):
            return lax.dynamic_slice(record, (jnp.zeros((), jnp.int32), start.astype(jnp.int32)), (CHANNELS, seg_len))
        return jax.vmap(cut_window)(offsets_day)
    segments = jax.vmap(cut_day)(records, window_offsets)
    white = whiten(segments, filter_taps)
    blocks = jnp.transpose(white, (2, 0, 1, 3)).reshape(blocks_count, C_BLK, DAYS, WIN, L)
    padded = jnp.pad(blocks, ((0, 0), (0, 0), (0, 0), (0, 0), (MAXLAG, MAXLAG)))
    results = []
    for round_index in range(ROUNDS):
        mask_value = pair_masks[round_index]

        def one_block(block_index):
            mine = blocks[block_index].astype(jnp.float32)
            theirs = padded[jnp.bitwise_xor(block_index, mask_value)].astype(jnp.float32)

            def one_lag(lag_index):
                shifted = lax.dynamic_slice_in_dim(theirs, lag_index, L, axis=3)
                return jnp.einsum('cxwt,dxwt->cd', mine, shifted, precision=lax.Precision.HIGHEST)
            return lax.map(one_lag, jnp.arange(LAGS, dtype=jnp.int32))
        tables = lax.map(one_block, jnp.arange(blocks_count, dtype=jnp.int32))
        tables = jnp.transpose(tables, (1, 0, 2, 3)).reshape(LAGS, CHANNELS * C_BLK)
        results.append(tables)
    norm_factor = 1.0 / jnp.sqrt(jnp.float32(DAYS * WIN * L))
    return jnp.stack(results) * norm_factor
```

```python
import functools

import jax
import jax.numpy as jnp
from jax import lax
from jax.experimental import pallas as pl
from jax.experimental.pallas import tpu as pltpu
from jax.sharding import PartitionSpec as P

MESH = pl.DeviceIdType.MESH
F32, BF16 = jnp.float32, jnp.bfloat16
NT = (((1,), (1,)), ((), ()))

L, MAXLAG, TAPS = 1024, 32, 64
LAGS = 2 * MAXLAG + 1
CH = 64
STEP = 16
DELAYS = STEP + 1
GAP = 128
ROW = 2 * (L + GAP)
RING = 4
XR = DELAYS * STEP
XH = 144
ZR = 80
ZH = 48


def whiten_kernel(offsets, record, taps, white, band):
    width = 384
    band[...] = jnp.zeros_like(band)
    band[0:1, 0:TAPS] = taps[...].astype(F32)
    rows = jnp.broadcast_to(band[0:1, :], (256, width))
    toeplitz = pltpu.roll(rows, 0, 1, stride=1, stride_axis=0).astype(BF16)
    span = 1280
    last = (record.shape[1] - span) // 128
    for w in range(2):
        start = offsets[0, w]
        tile = jnp.minimum(start // 128, last)
        base = pl.multiple_of(tile * 128, 128)
        data = record[:, pl.ds(base, span)].astype(F32)
        data = pltpu.roll(data, span - (start - base), 1).astype(BF16)
        parts = jnp.concatenate([data[:, 256 * m : 256 * m + width] for m in range(4)], axis=0)
        total = lax.dot_general(parts, toeplitz, NT, preferred_element_type=F32)
        square = jnp.sum(total * total, axis=1, keepdims=True)
        power = sum(square[CH * m : CH * (m + 1)] for m in range(4)) / L
        scale = lax.rsqrt(power + 1e-06)
        for m in range(4):
            lanes = slice(L * w + 256 * m, L * w + 256 * (m + 1))
            white[:, lanes] = (total[CH * m : CH * (m + 1)] * scale).astype(BF16)


def gapped(block):
    zeros = jnp.zeros((CH, GAP), BF16)
    return jnp.concatenate([block[:, :L], zeros, block[:, L:], zeros], axis=1)


class Ring:
    def __init__(self, half, right, left, far, near_r, near_l, hop_r, hop_l, got_l, got_r, send, recv):
        self.half = half
        self.right, self.left = right, left
        self.far, self.near_r, self.near_l = far, near_r, near_l
        self.hop_r, self.hop_l, self.got_l, self.got_r = hop_r, hop_l, got_l, got_r
        self.send, self.recv = send, recv

    def copy(self, r, k):
        lo, hi = pl.ds(0, self.half), pl.ds(self.half, self.far.shape[1] - self.half)
        src, dst, to = (
            (self.far.at[r, lo], self.hop_r.at[r], self.right),
            (self.far.at[r, hi], self.hop_l.at[r], self.left),
            (self.near_r.at[r, hi], self.got_l.at[r, hi], self.right),
            (self.near_l.at[r, lo], self.got_r.at[r, lo], self.left),
            (self.near_r.at[r, lo], self.got_l.at[r, lo], self.right),
            (self.near_l.at[r, hi], self.got_r.at[r, hi], self.left),
        )[k]
        return pltpu.make_async_remote_copy(
            src_ref=src, dst_ref=dst, send_sem=self.send.at[r, k], recv_sem=self.recv.at[r, k],
            device_id={"day": to}, device_id_type=MESH,
        )


def reduce_kernel(
    own, p0, p1, p2, out,
    astack, bstack, c_own, c_r, c_l, s_buf, z_buf,
    x_far, x_r, x_l, x_hr, x_hl, x_gl, x_gr, xs, xd,
    z_far, z_r, z_l, z_hr, z_hl, z_gl, z_gr, zs, zd,
):
    day = lax.axis_index("day")
    x, zh = day // RING, day % RING
    x_right, x_left = ((x + 1) % RING) * RING + zh, ((x + 3) % RING) * RING + zh
    z_right, z_left = x * RING + (zh + 1) % RING, x * RING + (zh + 3) % RING
    barrier = pltpu.get_barrier_semaphore()
    for other in (x_right, x_left, z_right, z_left):
        pl.semaphore_signal(barrier, inc=1, device_id={"day": other}, device_id_type=MESH)

    xring = Ring(XH, x_right, x_left, x_far, x_r, x_l, x_hr, x_hl, x_gl, x_gr, xs, xd)
    zring = Ring(ZH, z_right, z_left, z_far, z_r, z_l, z_hr, z_hl, z_gl, z_gr, zs, zd)

    mine = gapped(own[...])
    for a in range(DELAYS):
        moved = pltpu.roll(mine, a, 1) if a else mine
        for part in range(RING):
            astack[part, 16 * a : 16 * a + 16, :] = moved[16 * part : 16 * part + 16]
    pl.semaphore_wait(barrier, 4)

    norm = 1.0 / jnp.sqrt(jnp.float32(16 * 2 * L))

    def product(part):
        return lax.dot_general(astack[part], bstack[...], NT, preferred_element_type=F32)

    def compute(r):
        theirs = gapped((p0, p1, p2)[r][...])
        for b in range(4):
            shift = (MAXLAG - STEP * b) % ROW
            bstack[CH * b : CH * (b + 1), :] = pltpu.roll(theirs, shift, 1) if shift else theirs
        x_far[r] = product((x + 2) % RING).astype(BF16)
        xring.copy(r, 0).start()
        xring.copy(r, 1).start()
        piece = product((x + 1) % RING)
        x_r[r, XH:, :] = piece[XH:].astype(BF16)
        xring.copy(r, 2).start()
        c_r[r] = piece[:XH]
        piece = product((x + 3) % RING)
        x_l[r, :XH, :] = piece[:XH].astype(BF16)
        xring.copy(r, 3).start()
        c_l[r] = piece[XH:]
        c_own[r] = product(x)

    def x_merge(r):
        xring.copy(r, 0).wait_recv()
        x_r[r, :XH, :] = (c_r[r] + x_hr[r].astype(F32)).astype(BF16)
        xring.copy(r, 4).start()
        xring.copy(r, 1).wait_recv()
        x_l[r, XH:, :] = (c_l[r] + x_hl[r].astype(F32)).astype(BF16)
        xring.copy(r, 5).start()

    def x_end(r):
        for k in (2, 3, 4, 5):
            xring.copy(r, k).wait_recv()
        total = c_own[r] + x_gl[r].astype(F32) + x_gr[r].astype(F32)
        for h in range(2):
            s_buf[h] = total[:, 128 * h : 128 * (h + 1)]
        for part in range(RING):
            for i in range(4):
                for h in range(2):
                    z_buf[r, part, 16 * i : 16 * i + 16, 128 * h : 128 * (h + 1)] = s_buf[
                        h, pl.ds(4 * part + i, 16, stride=16), :
                    ]
            z_buf[r, part, 64:80, :] = total[256:272]
        z_far[r] = z_buf[r, (zh + 2) % RING].astype(BF16)
        zring.copy(r, 0).start()
        zring.copy(r, 1).start()
        z_r[r, ZH:, :] = z_buf[r, (zh + 1) % RING, ZH:, :].astype(BF16)
        zring.copy(r, 2).start()
        z_l[r, :ZH, :] = z_buf[r, (zh + 3) % RING, :ZH, :].astype(BF16)
        zring.copy(r, 3).start()

    def z_merge(r):
        zring.copy(r, 0).wait_recv()
        z_r[r, :ZH, :] = (z_buf[r, (zh + 1) % RING, :ZH, :] + z_hr[r].astype(F32)).astype(BF16)
        zring.copy(r, 4).start()
        zring.copy(r, 1).wait_recv()
        z_l[r, ZH:, :] = (z_buf[r, (zh + 3) % RING, ZH:, :] + z_hl[r].astype(F32)).astype(BF16)
        zring.copy(r, 5).start()

    def z_end(r):
        for k in (2, 3, 4, 5):
            zring.copy(r, k).wait_recv()
        total = (z_buf[r, zh] + z_gl[r].astype(F32) + z_gr[r].astype(F32)) * norm
        for b in range(4):
            cut = total[:64, CH * b : CH * (b + 1)]
            for pair in range(2):
                out[r, 16 * b : 16 * b + 16, 128 * pair : 128 * (pair + 1)] = jnp.concatenate(
                    [cut[32 * pair : 32 * pair + 16], cut[32 * pair + 16 : 32 * pair + 32]], axis=1
                )
        tail = total[64:68, 192:256]
        for part in range(1, RING):
            tail = jnp.where(zh == part, total[64 + 4 * part : 68 + 4 * part, 192:256], tail)
        out[r, 64:65, :] = jnp.concatenate([tail[i : i + 1] for i in range(4)], axis=1)

    compute(0)
    compute(1)
    x_merge(0)
    compute(2)
    x_end(0)
    x_merge(1)
    z_merge(0)
    x_end(1)
    x_merge(2)
    z_merge(1)
    x_end(2)
    z_end(0)
    z_merge(2)
    z_end(1)
    z_end(2)
    for r in range(3):
        for k in range(6):
            xring.copy(r, k).wait_send()
            zring.copy(r, k).wait_send()


def ring_scratch(rows, half):
    full = pltpu.VMEM((3, rows, 256), BF16)
    return [
        full, full, full,
        pltpu.VMEM((3, half, 256), BF16), pltpu.VMEM((3, rows - half, 256), BF16),
        full, full,
        pltpu.SemaphoreType.DMA((3, 6)), pltpu.SemaphoreType.DMA((3, 6)),
    ]


def partner(value, mask):
    count = lax.axis_size("chan")
    return lax.ppermute(value, "chan", [(i, i ^ mask) for i in range(count)])


def local(records, filter_taps, window_offsets, pair_masks):
    vmem = pl.BlockSpec(memory_space=pltpu.VMEM)
    white = pl.pallas_call(
        whiten_kernel,
        out_shape=jax.ShapeDtypeStruct((CH, 2 * L), BF16),
        in_specs=[pl.BlockSpec(memory_space=pltpu.SMEM), vmem, vmem],
        out_specs=vmem,
        scratch_shapes=[pltpu.VMEM((8, 384), F32)],
        compiler_params=pltpu.CompilerParams(vmem_limit_bytes=16 << 20),
        name="whiten",
    )(window_offsets, records[0], filter_taps[None])

    count = lax.axis_size("chan")
    middle = jnp.sum(pair_masks) - count
    near = partner(white, 1)
    far = partner(white, count - 1)
    other = lax.switch(middle - 2, [functools.partial(partner, mask=m) for m in range(2, count - 1)], white)

    res = pl.pallas_call(
        reduce_kernel,
        out_shape=jax.ShapeDtypeStruct((3, LAGS, 256), F32),
        in_specs=[vmem] * 4,
        out_specs=vmem,
        scratch_shapes=[
            pltpu.VMEM((RING, XR, ROW), BF16),
            pltpu.VMEM((4 * CH, ROW), BF16),
            pltpu.VMEM((3, XR, 256), F32),
            pltpu.VMEM((3, XH, 256), F32),
            pltpu.VMEM((3, XR - XH, 256), F32),
            pltpu.VMEM((2, XR, 128), F32),
            pltpu.VMEM((3, RING, ZR, 256), F32),
            *ring_scratch(XR, XH),
            *ring_scratch(ZR, ZH),
        ],
        compiler_params=pltpu.CompilerParams(collective_id=0, has_side_effects=True, vmem_limit_bytes=48 << 20),
        name="correlate",
    )(white, near, far, other)
    kind = pair_masks[:, None, None]
    return jnp.where(kind == 1, res[0], jnp.where(kind == count - 1, res[1], res[2]))


def solution(mesh):
    in_specs = (P("day", "chan", None), P(), P("day", None), P())
    out_specs = P(None, None, ("chan", "day"))
    return jax.shard_map(local, mesh=mesh, in_specs=in_specs, out_specs=out_specs, check_vma=False)
```

```python
import functools

import jax
import jax.numpy as jnp
from jax import lax
from jax.experimental import pallas as pl
from jax.experimental.pallas import tpu as pltpu
from jax.sharding import PartitionSpec as P

MESH = pl.DeviceIdType.MESH
F32, BF16 = jnp.float32, jnp.bfloat16
NT = (((1,), (1,)), ((), ()))

L, MAXLAG, TAPS = 1024, 32, 64
LAGS = 2 * MAXLAG + 1
CH = 64
STEP = 16
DELAYS = STEP + 1
GAP = 128
ROW = 2 * (L + GAP)
RING = 4
XR = DELAYS * STEP
ZR = 4 * STEP
PART = 64
SPLIT = CH // PART
CHUNKS = 3 * SPLIT
WIDE = 4 * PART
X_MERGED = (0, 1)
Z_MERGED = (0, 1)
ORDER = ("C0", "C1", "M0", "M1", "X0", "C2", "X1", "N0", "N1", "X2", "Z0", "Z1", "Z2")
LAST = f"X{CHUNKS - 1}"


def whiten_kernel(offsets, record, taps, white, band):
    width = 384
    band[...] = jnp.zeros_like(band)
    band[0:1, 0:TAPS] = taps[...].astype(F32)
    rows = jnp.broadcast_to(band[0:1, :], (256, width))
    toeplitz = pltpu.roll(rows, 0, 1, stride=1, stride_axis=0).astype(BF16)
    span = 1280
    last = (record.shape[1] - span) // 128
    for w in range(2):
        start = offsets[0, w]
        tile = jnp.minimum(start // 128, last)
        base = pl.multiple_of(tile * 128, 128)
        data = record[:, pl.ds(base, span)].astype(F32)
        data = pltpu.roll(data, span - (start - base), 1).astype(BF16)
        parts = jnp.concatenate([data[:, 256 * m : 256 * m + width] for m in range(4)], axis=0)
        total = lax.dot_general(parts, toeplitz, NT, preferred_element_type=F32)
        square = jnp.sum(total * total, axis=1, keepdims=True)
        power = sum(square[CH * m : CH * (m + 1)] for m in range(4)) / L
        scale = lax.rsqrt(power + 1e-06)
        for m in range(4):
            lanes = slice(L * w + 256 * m, L * w + 256 * (m + 1))
            white[:, lanes] = (total[CH * m : CH * (m + 1)] * scale).astype(BF16)


def gapped(block):
    zeros = jnp.zeros((block.shape[0], GAP), BF16)
    return jnp.concatenate([block[:, :L], zeros, block[:, L:], zeros], axis=1)


class Ring:
    def __init__(self, right, left, far, to_r, to_l, to_f, hop_r, hop_l, got_r, got_l, got_f, send, recv):
        self.right, self.left, self.far = right, left, far
        self.to_r, self.to_l, self.to_f, self.hop_r, self.hop_l = to_r, to_l, to_f, hop_r, hop_l
        self.got_r, self.got_l, self.got_f = got_r, got_l, got_f
        self.send, self.recv = send, recv
        self.half = to_r.shape[1] // 2 // 16 * 16

    def copy(self, c, k, merged):
        if merged:
            lo, hi = pl.ds(0, self.half), pl.ds(self.half, self.to_r.shape[1] - self.half)
            src, dst, to = (
                (self.to_f.at[c, lo], self.hop_r.at[c], self.right),
                (self.to_f.at[c, hi], self.hop_l.at[c], self.left),
                (self.to_r.at[c, hi], self.got_l.at[c, hi], self.right),
                (self.to_l.at[c, lo], self.got_r.at[c, lo], self.left),
                (self.to_r.at[c, lo], self.got_l.at[c, lo], self.right),
                (self.to_l.at[c, hi], self.got_r.at[c, hi], self.left),
            )[k]
        else:
            src, dst, to = (
                (self.to_f.at[c], self.got_f.at[c], self.far),
                (self.to_r.at[c], self.got_l.at[c], self.right),
                (self.to_l.at[c], self.got_r.at[c], self.left),
            )[k]
        return pltpu.make_async_remote_copy(
            src_ref=src, dst_ref=dst, send_sem=self.send.at[c, k], recv_sem=self.recv.at[c, k],
            device_id={"day": to}, device_id_type=MESH,
        )


def reduce_kernel(
    own, middle, out,
    astack, bstack, near, distant, c_own, c_r, c_l, s_buf, z_buf, t_buf, e_own, e_send, e_got,
    x_r, x_l, x_f, x_hr, x_hl, x_gr, x_gl, x_gf, xs, xd,
    z_r, z_l, z_f, z_hr, z_hl, z_gr, z_gl, z_gf, zs, zd,
    es, ed, ps, pd,
):
    day, chan = lax.axis_index("day"), lax.axis_index("chan")
    x, zh = day // RING, day % RING
    x_to = [((x + k) % RING) * RING + zh for k in range(RING)]
    z_to = [x * RING + (zh + k) % RING for k in range(RING)]
    near_to = chan + 1 - 2 * (chan % 2)
    far_to = lax.axis_size("chan") - 1 - chan
    barrier = pltpu.get_barrier_semaphore()
    for other in (*x_to[1:], *z_to[1:]):
        pl.semaphore_signal(barrier, inc=1, device_id={"day": other}, device_id_type=MESH)
    for other in (near_to, far_to):
        pl.semaphore_signal(barrier, inc=1, device_id={"chan": other}, device_id_type=MESH)

    xring = Ring(x_to[1], x_to[3], x_to[2], x_r, x_l, x_f, x_hr, x_hl, x_gr, x_gl, x_gf, xs, xd)
    zring = Ring(z_to[1], z_to[3], z_to[2], z_r, z_l, z_f, z_hr, z_hl, z_gr, z_gl, z_gf, zs, zd)

    def block_copy(k, h):
        rows = pl.ds(PART * h, PART)
        return pltpu.make_async_remote_copy(
            src_ref=own.at[rows], dst_ref=(near, distant)[k].at[rows], send_sem=ps.at[k, h], recv_sem=pd.at[k, h],
            device_id={"chan": (near_to, far_to)[k]}, device_id_type=MESH,
        )

    mine = gapped(own[...])
    for a in range(DELAYS):
        moved = pltpu.roll(mine, a, 1) if a else mine
        for part in range(RING):
            astack[part, 16 * a : 16 * a + 16, :] = moved[16 * part : 16 * part + 16]

    pl.semaphore_wait(barrier, 8)
    for h in range(SPLIT):
        for k in range(2):
            block_copy(k, h).start()

    norm = 1.0 / jnp.sqrt(jnp.float32(16 * 2 * L))

    def product(k):
        return lax.dot_general(astack[(x + k) % RING], bstack[...], NT, preferred_element_type=F32)

    def compute(c):
        r, h = c // SPLIT, c % SPLIT
        if r:
            block_copy(r - 1, h).wait_recv()
        theirs = gapped((middle, near, distant)[r][PART * h : PART * (h + 1)])
        for b in range(4):
            shift = (MAXLAG - STEP * b) % ROW
            bstack[PART * b : PART * (b + 1), :] = pltpu.roll(theirs, shift, 1) if shift else theirs
        merged, half = c in X_MERGED, xring.half
        x_f[c] = product(2).astype(BF16)
        xring.copy(c, 0, merged).start()
        if merged:
            xring.copy(c, 1, True).start()
            piece = product(1)
            x_r[c, half:] = piece[half:].astype(BF16)
            xring.copy(c, 2, True).start()
            c_r[c] = piece[:half]
            piece = product(3)
            x_l[c, :half] = piece[:half].astype(BF16)
            xring.copy(c, 3, True).start()
            c_l[c] = piece[half:]
        else:
            x_r[c] = product(1).astype(BF16)
            xring.copy(c, 1, False).start()
            x_l[c] = product(3).astype(BF16)
            xring.copy(c, 2, False).start()
        c_own[c] = product(0)

    def x_merge(c):
        half = xring.half
        xring.copy(c, 0, True).wait_recv()
        x_r[c, :half] = (c_r[c] + x_hr[c].astype(F32)).astype(BF16)
        xring.copy(c, 4, True).start()
        xring.copy(c, 1, True).wait_recv()
        x_l[c, half:] = (c_l[c] + x_hl[c].astype(F32)).astype(BF16)
        xring.copy(c, 5, True).start()

    def x_end(c):
        merged = c in X_MERGED
        for k in range(2, 6) if merged else range(3):
            xring.copy(c, k, merged).wait_recv()
        total = c_own[c] + x_gl[c].astype(F32) + x_gr[c].astype(F32)
        if not merged:
            total += x_gf[c].astype(F32)
        for side in range(WIDE // 128):
            lanes = slice(128 * side, 128 * (side + 1))
            s_buf[side] = total[:, lanes]
            for part in range(RING):
                for i in range(4):
                    z_buf[c, part, 16 * i : 16 * i + 16, lanes] = s_buf[side, pl.ds(4 * part + i, 16, stride=16), :]
        e_own[:, PART * c : PART * (c + 1)] = total[256:272, 3 * PART :]
        merged = c in Z_MERGED
        z_f[c] = z_buf[c, (zh + 2) % RING].astype(BF16)
        if not merged:
            zring.copy(c, 0, merged).start()
            z_r[c] = z_buf[c, (zh + 1) % RING].astype(BF16)
            zring.copy(c, 1, merged).start()
            z_l[c] = z_buf[c, (zh + 3) % RING].astype(BF16)
            zring.copy(c, 2, merged).start()
        else:
            zring.copy(c, 0, merged).start()
            zring.copy(c, 1, merged).start()
            half = zring.half
            z_r[c, half:] = z_buf[c, (zh + 1) % RING, half:].astype(BF16)
            zring.copy(c, 2, merged).start()
            z_l[c, :half] = z_buf[c, (zh + 3) % RING, :half].astype(BF16)
            zring.copy(c, 3, merged).start()

    def z_merge(c):
        half = zring.half
        zring.copy(c, 0, True).wait_recv()
        z_r[c, :half] = (z_buf[c, (zh + 1) % RING, :half] + z_hr[c].astype(F32)).astype(BF16)
        zring.copy(c, 4, True).start()
        zring.copy(c, 1, True).wait_recv()
        z_l[c, half:] = (z_buf[c, (zh + 3) % RING, half:] + z_hl[c].astype(F32)).astype(BF16)
        zring.copy(c, 5, True).start()

    def z_end(c):
        merged = c in Z_MERGED
        for k in range(2, 6) if merged else range(3):
            zring.copy(c, k, merged).wait_recv()
        total = z_buf[c, zh] + z_gl[c].astype(F32) + z_gr[c].astype(F32)
        if not merged:
            total += z_gf[c].astype(F32)
        t_buf[c] = total * norm
        if c % SPLIT == SPLIT - 1:
            first = c + 1 - SPLIT
            for b in range(4):
                cut = [t_buf[first + h, :, PART * b : PART * (b + 1)] for h in range(SPLIT)]
                out[c // SPLIT, 16 * b : 16 * b + 16, :] = jnp.concatenate(
                    [cut[h][16 * i : 16 * i + 16] for i in range(4) for h in range(SPLIT)], axis=1
                )

    def e_copy(k):
        return pltpu.make_async_remote_copy(
            src_ref=e_send, dst_ref=e_got.at[k - 1], send_sem=es.at[k - 1], recv_sem=ed.at[k - 1],
            device_id={"day": z_to[k]}, device_id_type=MESH,
        )

    steps = {"C": compute, "M": x_merge, "X": x_end, "N": z_merge, "Z": z_end}
    for step in ORDER:
        steps[step[0]](int(step[1:]))
        if step == LAST:
            e_send[...] = e_own[...].astype(BF16)
            for k in range(1, RING):
                e_copy(k).start()

    for k in range(1, RING):
        e_copy(k).wait_recv()
    tails = (e_own[...] + sum(e_got[k].astype(F32) for k in range(3))) * norm
    tail = tails[0:4]
    for part in range(1, RING):
        tail = jnp.where(zh == part, tails[4 * part : 4 * part + 4], tail)
    for r in range(3):
        out[r, 64:65, :] = jnp.concatenate([tail[i : i + 1, CH * r : CH * (r + 1)] for i in range(4)], axis=1)

    for k in range(1, RING):
        e_copy(k).wait_send()
    for k in range(2):
        for h in range(SPLIT):
            block_copy(k, h).wait_send()
    for c in range(CHUNKS):
        for k in range(6 if c in X_MERGED else 3):
            xring.copy(c, k, c in X_MERGED).wait_send()
        for k in range(6 if c in Z_MERGED else 3):
            zring.copy(c, k, c in Z_MERGED).wait_send()


def partner(value, mask):
    count = lax.axis_size("chan")
    return lax.ppermute(value, "chan", [(i, i ^ mask) for i in range(count)])


def correlate(white, other):
    def chunks(rows, kind=BF16):
        return pltpu.VMEM((CHUNKS, rows, WIDE), kind)

    def sems(*shape):
        return pltpu.SemaphoreType.DMA(shape)

    vmem = pl.BlockSpec(memory_space=pltpu.VMEM)
    return pl.pallas_call(
        reduce_kernel,
        out_shape=jax.ShapeDtypeStruct((3, LAGS, 256), F32),
        in_specs=[vmem] * 2,
        out_specs=vmem,
        scratch_shapes=[
            pltpu.VMEM((RING, XR, ROW), BF16),
            pltpu.VMEM((WIDE, ROW), BF16),
            pltpu.VMEM((CH, 2 * L), BF16),
            pltpu.VMEM((CH, 2 * L), BF16),
            chunks(XR, F32),
            chunks(XR // 32 * 16, F32),
            chunks(XR - XR // 32 * 16, F32),
            pltpu.VMEM((WIDE // 128, XR, 128), F32),
            pltpu.VMEM((CHUNKS, RING, ZR, WIDE), F32),
            chunks(ZR, F32),
            pltpu.VMEM((16, CHUNKS * PART), F32),
            pltpu.VMEM((16, CHUNKS * PART), BF16),
            pltpu.VMEM((3, 16, CHUNKS * PART), BF16),
            *[chunks(XR) for _ in range(3)],
            chunks(XR // 32 * 16),
            chunks(XR - XR // 32 * 16),
            *[chunks(XR) for _ in range(3)],
            sems(CHUNKS, 6), sems(CHUNKS, 6),
            *[chunks(ZR) for _ in range(3)],
            *[chunks(ZR // 2) for _ in range(2)],
            *[chunks(ZR) for _ in range(3)],
            sems(CHUNKS, 6), sems(CHUNKS, 6),
            sems(3), sems(3),
            sems(2, SPLIT), sems(2, SPLIT),
        ],
        compiler_params=pltpu.CompilerParams(collective_id=0, has_side_effects=True, vmem_limit_bytes=48 << 20),
        name="correlate",
    )(white, other)


def local(records, filter_taps, window_offsets, pair_masks):
    vmem = pl.BlockSpec(memory_space=pltpu.VMEM)
    white = pl.pallas_call(
        whiten_kernel,
        out_shape=jax.ShapeDtypeStruct((CH, 2 * L), BF16),
        in_specs=[pl.BlockSpec(memory_space=pltpu.SMEM), vmem, vmem],
        out_specs=vmem,
        scratch_shapes=[pltpu.VMEM((8, 384), F32)],
        compiler_params=pltpu.CompilerParams(vmem_limit_bytes=16 << 20),
        name="whiten",
    )(window_offsets, records[0], filter_taps[None])

    count = lax.axis_size("chan")
    middle = jnp.sum(pair_masks) - count
    other = lax.switch(middle - 2, [functools.partial(partner, mask=m) for m in range(2, count - 1)], white)

    res = correlate(white, other)
    kind = pair_masks[:, None, None]
    return jnp.where(kind == 1, res[1], jnp.where(kind == count - 1, res[2], res[0]))


def solution(mesh):
    in_specs = (P("day", "chan", None), P(), P("day", None), P())
    out_specs = P(None, None, ("chan", "day"))
    return jax.shard_map(local, mesh=mesh, in_specs=in_specs, out_specs=out_specs, check_vma=False)
```

```python
import functools

import jax
import jax.numpy as jnp
from jax import lax
from jax.experimental import pallas as pl
from jax.experimental.pallas import tpu as pltpu
from jax.sharding import PartitionSpec as P

MESH = pl.DeviceIdType.MESH
F32, BF16 = jnp.float32, jnp.bfloat16
NT = (((1,), (1,)), ((), ()))

L, MAXLAG, TAPS = 1024, 32, 64
LAGS = 2 * MAXLAG + 1
CH = 64
STEP = 16
DELAYS = STEP + 1
GAP = 128
ROW = 2 * (L + GAP)
RING = 4
XR = DELAYS * STEP
ZR = 4 * STEP
PART = 64
SPLIT = CH // PART
CHUNKS = 3 * SPLIT
WIDE = 4 * PART
X_MERGED = (0, 1)
Z_MERGED = (0, 1)
ORDER = ("C1", "M0", "M1", "X0", "C2", "X1", "N0", "N1", "X2", "Z0", "Z1", "Z2")
LAST = f"X{CHUNKS - 1}"


def whiten_kernel(offsets, record, taps, white, band):
    width = 384
    band[...] = jnp.zeros_like(band)
    band[0:1, 0:TAPS] = taps[...].astype(F32)
    rows = jnp.broadcast_to(band[0:1, :], (256, width))
    toeplitz = pltpu.roll(rows, 0, 1, stride=1, stride_axis=0).astype(BF16)
    span = 1280
    last = (record.shape[1] - span) // 128
    for w in range(2):
        start = offsets[0, w]
        tile = jnp.minimum(start // 128, last)
        base = pl.multiple_of(tile * 128, 128)
        data = record[:, pl.ds(base, span)].astype(F32)
        data = pltpu.roll(data, span - (start - base), 1).astype(BF16)
        parts = jnp.concatenate([data[:, 256 * m : 256 * m + width] for m in range(4)], axis=0)
        total = lax.dot_general(parts, toeplitz, NT, preferred_element_type=F32)
        square = jnp.sum(total * total, axis=1, keepdims=True)
        power = sum(square[CH * m : CH * (m + 1)] for m in range(4)) / L
        scale = lax.rsqrt(power + 1e-06)
        for m in range(4):
            lanes = slice(L * w + 256 * m, L * w + 256 * (m + 1))
            white[:, lanes] = (total[CH * m : CH * (m + 1)] * scale).astype(BF16)


def gapped(block):
    zeros = jnp.zeros((block.shape[0], GAP), BF16)
    return jnp.concatenate([block[:, :L], zeros, block[:, L:], zeros], axis=1)


class Ring:
    def __init__(self, right, left, far, to_r, to_l, to_f, hop_r, hop_l, got_r, got_l, got_f, send, recv):
        self.right, self.left, self.far = right, left, far
        self.to_r, self.to_l, self.to_f, self.hop_r, self.hop_l = to_r, to_l, to_f, hop_r, hop_l
        self.got_r, self.got_l, self.got_f = got_r, got_l, got_f
        self.send, self.recv = send, recv
        self.half = to_r.shape[1] // 2 // 16 * 16

    def copy(self, c, k, merged):
        if merged:
            lo, hi = pl.ds(0, self.half), pl.ds(self.half, self.to_r.shape[1] - self.half)
            src, dst, to = (
                (self.to_f.at[c, lo], self.hop_r.at[c], self.right),
                (self.to_f.at[c, hi], self.hop_l.at[c], self.left),
                (self.to_r.at[c, hi], self.got_l.at[c, hi], self.right),
                (self.to_l.at[c, lo], self.got_r.at[c, lo], self.left),
                (self.to_r.at[c, lo], self.got_l.at[c, lo], self.right),
                (self.to_l.at[c, hi], self.got_r.at[c, hi], self.left),
            )[k]
        else:
            src, dst, to = (
                (self.to_f.at[c], self.got_f.at[c], self.far),
                (self.to_r.at[c], self.got_l.at[c], self.right),
                (self.to_l.at[c], self.got_r.at[c], self.left),
            )[k]
        return pltpu.make_async_remote_copy(
            src_ref=src, dst_ref=dst, send_sem=self.send.at[c, k], recv_sem=self.recv.at[c, k],
            device_id={"day": to}, device_id_type=MESH,
        )


def reduce_kernel(
    own, middle, near, out,
    astack, bstack, distant, c_own, c_r, c_l, s_buf, z_buf, t_buf, e_own, e_send, e_got,
    x_r, x_l, x_f, x_hr, x_hl, x_gr, x_gl, x_gf, xs, xd,
    z_r, z_l, z_f, z_hr, z_hl, z_gr, z_gl, z_gf, zs, zd,
    es, ed, ps, pd,
):
    day, chan = lax.axis_index("day"), lax.axis_index("chan")
    x, zh = day // RING, day % RING
    x_to = [((x + k) % RING) * RING + zh for k in range(RING)]
    z_to = [x * RING + (zh + k) % RING for k in range(RING)]
    far_to = lax.axis_size("chan") - 1 - chan
    barrier = pltpu.get_barrier_semaphore()
    for other in (*x_to[1:], *z_to[1:]):
        pl.semaphore_signal(barrier, inc=1, device_id={"day": other}, device_id_type=MESH)
    pl.semaphore_signal(barrier, inc=1, device_id={"chan": far_to}, device_id_type=MESH)

    xring = Ring(x_to[1], x_to[3], x_to[2], x_r, x_l, x_f, x_hr, x_hl, x_gr, x_gl, x_gf, xs, xd)
    zring = Ring(z_to[1], z_to[3], z_to[2], z_r, z_l, z_f, z_hr, z_hl, z_gr, z_gl, z_gf, zs, zd)

    def block_copy(h):
        rows = pl.ds(PART * h, PART)
        return pltpu.make_async_remote_copy(
            src_ref=own.at[rows], dst_ref=distant.at[rows], send_sem=ps.at[h], recv_sem=pd.at[h],
            device_id={"chan": far_to}, device_id_type=MESH,
        )

    mine = gapped(own[...])
    for a in range(DELAYS):
        moved = pltpu.roll(mine, a, 1) if a else mine
        for part in range(RING):
            astack[part, 16 * a : 16 * a + 16, :] = moved[16 * part : 16 * part + 16]

    norm = 1.0 / jnp.sqrt(jnp.float32(16 * 2 * L))

    def product(k):
        return lax.dot_general(astack[(x + k) % RING], bstack[...], NT, preferred_element_type=F32)

    def compute(c, start=True):
        r, h = c // SPLIT, c % SPLIT
        merged, half = c in X_MERGED, xring.half
        if r == 2:
            block_copy(h).wait_recv()
        theirs = gapped((middle, near, distant)[r][PART * h : PART * (h + 1)])
        for b in range(4):
            shift = (MAXLAG - STEP * b) % ROW
            bstack[PART * b : PART * (b + 1), :] = pltpu.roll(theirs, shift, 1) if shift else theirs
        x_f[c] = product(2).astype(BF16)
        if start:
            x_start(c, (0, 1) if merged else (0,))
        piece = product(1)
        if merged:
            x_r[c, half:] = piece[half:].astype(BF16)
            c_r[c] = piece[:half]
        else:
            x_r[c] = piece.astype(BF16)
        if start:
            x_start(c, (2,) if merged else (1,))
        piece = product(3)
        if merged:
            x_l[c, :half] = piece[:half].astype(BF16)
            c_l[c] = piece[half:]
        else:
            x_l[c] = piece.astype(BF16)
        if start:
            x_start(c, (3,) if merged else (2,))
        c_own[c] = product(0)

    def x_start(c, which):
        for k in which:
            xring.copy(c, k, c in X_MERGED).start()

    def x_merge(c):
        half = xring.half
        xring.copy(c, 0, True).wait_recv()
        x_r[c, :half] = (c_r[c] + x_hr[c].astype(F32)).astype(BF16)
        xring.copy(c, 4, True).start()
        xring.copy(c, 1, True).wait_recv()
        x_l[c, half:] = (c_l[c] + x_hl[c].astype(F32)).astype(BF16)
        xring.copy(c, 5, True).start()

    def x_end(c):
        merged = c in X_MERGED
        for k in range(2, 6) if merged else range(3):
            xring.copy(c, k, merged).wait_recv()
        total = c_own[c] + x_gl[c].astype(F32) + x_gr[c].astype(F32)
        if not merged:
            total += x_gf[c].astype(F32)
        for side in range(WIDE // 128):
            lanes = slice(128 * side, 128 * (side + 1))
            s_buf[side] = total[:, lanes]
            for part in range(RING):
                for i in range(4):
                    z_buf[c, part, 16 * i : 16 * i + 16, lanes] = s_buf[side, pl.ds(4 * part + i, 16, stride=16), :]
        e_own[:, PART * c : PART * (c + 1)] = total[256:272, 3 * PART :]
        merged = c in Z_MERGED
        z_f[c] = z_buf[c, (zh + 2) % RING].astype(BF16)
        if not merged:
            zring.copy(c, 0, merged).start()
            z_r[c] = z_buf[c, (zh + 1) % RING].astype(BF16)
            zring.copy(c, 1, merged).start()
            z_l[c] = z_buf[c, (zh + 3) % RING].astype(BF16)
            zring.copy(c, 2, merged).start()
        else:
            zring.copy(c, 0, merged).start()
            zring.copy(c, 1, merged).start()
            half = zring.half
            z_r[c, half:] = z_buf[c, (zh + 1) % RING, half:].astype(BF16)
            zring.copy(c, 2, merged).start()
            z_l[c, :half] = z_buf[c, (zh + 3) % RING, :half].astype(BF16)
            zring.copy(c, 3, merged).start()

    def z_merge(c):
        half = zring.half
        zring.copy(c, 0, True).wait_recv()
        z_r[c, :half] = (z_buf[c, (zh + 1) % RING, :half] + z_hr[c].astype(F32)).astype(BF16)
        zring.copy(c, 4, True).start()
        zring.copy(c, 1, True).wait_recv()
        z_l[c, half:] = (z_buf[c, (zh + 3) % RING, half:] + z_hl[c].astype(F32)).astype(BF16)
        zring.copy(c, 5, True).start()

    def z_end(c):
        merged = c in Z_MERGED
        for k in range(2, 6) if merged else range(3):
            zring.copy(c, k, merged).wait_recv()
        total = z_buf[c, zh] + z_gl[c].astype(F32) + z_gr[c].astype(F32)
        if not merged:
            total += z_gf[c].astype(F32)
        t_buf[c] = total * norm
        if c % SPLIT == SPLIT - 1:
            first = c + 1 - SPLIT
            for b in range(4):
                cut = [t_buf[first + h, :, PART * b : PART * (b + 1)] for h in range(SPLIT)]
                out[c // SPLIT, 16 * b : 16 * b + 16, :] = jnp.concatenate(
                    [cut[h][16 * i : 16 * i + 16] for i in range(4) for h in range(SPLIT)], axis=1
                )

    def e_copy(k):
        return pltpu.make_async_remote_copy(
            src_ref=e_send, dst_ref=e_got.at[k - 1], send_sem=es.at[k - 1], recv_sem=ed.at[k - 1],
            device_id={"day": z_to[k]}, device_id_type=MESH,
        )

    steps = {"C": compute, "M": x_merge, "X": x_end, "N": z_merge, "Z": z_end}
    compute(0, start=False)
    pl.semaphore_wait(barrier, 7)
    for h in range(SPLIT):
        block_copy(h).start()
    x_start(0, range(4) if 0 in X_MERGED else range(3))
    for step in ORDER:
        steps[step[0]](int(step[1:]))
        if step == LAST:
            e_send[...] = e_own[...].astype(BF16)
            for k in range(1, RING):
                e_copy(k).start()

    for k in range(1, RING):
        e_copy(k).wait_recv()
    tails = (e_own[...] + sum(e_got[k].astype(F32) for k in range(3))) * norm
    tail = tails[0:4]
    for part in range(1, RING):
        tail = jnp.where(zh == part, tails[4 * part : 4 * part + 4], tail)
    for r in range(3):
        out[r, 64:65, :] = jnp.concatenate([tail[i : i + 1, CH * r : CH * (r + 1)] for i in range(4)], axis=1)

    for k in range(1, RING):
        e_copy(k).wait_send()
    for h in range(SPLIT):
        block_copy(h).wait_send()
    for c in range(CHUNKS):
        for k in range(6 if c in X_MERGED else 3):
            xring.copy(c, k, c in X_MERGED).wait_send()
        for k in range(6 if c in Z_MERGED else 3):
            zring.copy(c, k, c in Z_MERGED).wait_send()


def exchange_kernel(mask, own, middle, near, send, recv):
    chan, count = lax.axis_index("chan"), lax.axis_size("chan")
    flip = sum((1 - 2 * (chan // 2**k % 2)) * 2**k for k in range(count.bit_length() - 1) if mask >> k & 1)
    to = (chan + flip, chan + 1 - 2 * (chan % 2))
    barrier = pltpu.get_barrier_semaphore()
    for other in to:
        pl.semaphore_signal(barrier, inc=1, device_id={"chan": other}, device_id_type=MESH)
    pl.semaphore_wait(barrier, 2)
    copies = [
        pltpu.make_async_remote_copy(
            src_ref=own, dst_ref=dst, send_sem=send.at[k], recv_sem=recv.at[k],
            device_id={"chan": to[k]}, device_id_type=MESH,
        )
        for k, dst in enumerate((middle, near))
    ]
    for copy in copies:
        copy.start()
    for copy in copies:
        copy.wait()


def exchange(white, mask):
    vmem = pl.BlockSpec(memory_space=pltpu.VMEM)
    shape = jax.ShapeDtypeStruct(white.shape, white.dtype)
    return pl.pallas_call(
        functools.partial(exchange_kernel, mask),
        out_shape=(shape,) * 2,
        in_specs=[vmem],
        out_specs=(vmem,) * 2,
        scratch_shapes=[pltpu.SemaphoreType.DMA((2,)), pltpu.SemaphoreType.DMA((2,))],
        compiler_params=pltpu.CompilerParams(collective_id=mask, has_side_effects=True, vmem_limit_bytes=8 << 20),
        name=f"exchange{mask}",
    )(white)


def correlate(white, other, near):
    def chunks(rows, kind=BF16):
        return pltpu.VMEM((CHUNKS, rows, WIDE), kind)

    def sems(*shape):
        return pltpu.SemaphoreType.DMA(shape)

    vmem = pl.BlockSpec(memory_space=pltpu.VMEM)
    return pl.pallas_call(
        reduce_kernel,
        out_shape=jax.ShapeDtypeStruct((3, LAGS, 256), F32),
        in_specs=[vmem] * 3,
        out_specs=vmem,
        scratch_shapes=[
            pltpu.VMEM((RING, XR, ROW), BF16),
            pltpu.VMEM((WIDE, ROW), BF16),
            pltpu.VMEM((CH, 2 * L), BF16),
            chunks(XR, F32),
            chunks(XR // 32 * 16, F32),
            chunks(XR - XR // 32 * 16, F32),
            pltpu.VMEM((WIDE // 128, XR, 128), F32),
            pltpu.VMEM((CHUNKS, RING, ZR, WIDE), F32),
            chunks(ZR, F32),
            pltpu.VMEM((16, CHUNKS * PART), F32),
            pltpu.VMEM((16, CHUNKS * PART), BF16),
            pltpu.VMEM((3, 16, CHUNKS * PART), BF16),
            *[chunks(XR) for _ in range(3)],
            chunks(XR // 32 * 16),
            chunks(XR - XR // 32 * 16),
            *[chunks(XR) for _ in range(3)],
            sems(CHUNKS, 6), sems(CHUNKS, 6),
            *[chunks(ZR) for _ in range(3)],
            *[chunks(ZR // 2) for _ in range(2)],
            *[chunks(ZR) for _ in range(3)],
            sems(CHUNKS, 6), sems(CHUNKS, 6),
            sems(3), sems(3),
            sems(SPLIT), sems(SPLIT),
        ],
        compiler_params=pltpu.CompilerParams(collective_id=0, has_side_effects=True, vmem_limit_bytes=48 << 20),
        name="correlate",
    )(white, other, near)


def local(records, filter_taps, window_offsets, pair_masks):
    count = lax.axis_size("chan")
    middle = jnp.sum(pair_masks) - count
    vmem = pl.BlockSpec(memory_space=pltpu.VMEM)
    white = pl.pallas_call(
        whiten_kernel,
        out_shape=jax.ShapeDtypeStruct((CH, 2 * L), BF16),
        in_specs=[pl.BlockSpec(memory_space=pltpu.SMEM), vmem, vmem],
        out_specs=vmem,
        scratch_shapes=[pltpu.VMEM((8, 384), F32)],
        compiler_params=pltpu.CompilerParams(vmem_limit_bytes=16 << 20),
        name="whiten",
    )(window_offsets, records[0], filter_taps[None])

    branches = [functools.partial(exchange, mask=m) for m in range(2, count - 1)]
    other, near = lax.switch(middle - 2, branches, white)
    res = correlate(white, other, near)
    kind = pair_masks[:, None, None]
    return jnp.where(kind == 1, res[1], jnp.where(kind == count - 1, res[2], res[0]))


def solution(mesh):
    in_specs = (P("day", "chan", None), P(), P("day", None), P())
    out_specs = P(None, None, ("chan", "day"))
    return jax.shard_map(local, mesh=mesh, in_specs=in_specs, out_specs=out_specs, check_vma=False)
```

```python
import functools

import jax
import jax.numpy as jnp
from jax import lax
from jax.experimental import pallas as pl
from jax.experimental.pallas import tpu as pltpu
from jax.sharding import PartitionSpec as P

MESH = pl.DeviceIdType.MESH
F32, BF16 = jnp.float32, jnp.bfloat16
NT = (((1,), (1,)), ((), ()))

L, MAXLAG, TAPS = 1024, 32, 64
LAGS = 2 * MAXLAG + 1
CH = 64
STEP = 16
DELAYS = STEP + 1
GAP = 128
ROW = 2 * (L + GAP)
RING = 4
XR = DELAYS * STEP
ZR = 4 * STEP
PART = 64
SPLIT = CH // PART
CHUNKS = 3 * SPLIT
WIDE = 4 * PART
X_MERGED = (0, 1)
Z_MERGED = (0, 1)
ORDER = ("C1", "M0", "M1", "X0", "C2", "X1", "N0", "N1", "X2", "Z0", "Z1", "Z2")
LAST = f"X{CHUNKS - 1}"


def whiten_kernel(offsets, record, taps, white, band):
    width = 384
    band[...] = jnp.zeros_like(band)
    band[0:1, 0:TAPS] = taps[...].astype(F32)
    rows = jnp.broadcast_to(band[0:1, :], (256, width))
    toeplitz = pltpu.roll(rows, 0, 1, stride=1, stride_axis=0).astype(BF16)
    span = 1280
    last = (record.shape[1] - span) // 128
    for w in range(2):
        start = offsets[0, w]
        tile = jnp.minimum(start // 128, last)
        base = pl.multiple_of(tile * 128, 128)
        data = record[:, pl.ds(base, span)].astype(F32)
        data = pltpu.roll(data, span - (start - base), 1).astype(BF16)
        parts = jnp.concatenate([data[:, 256 * m : 256 * m + width] for m in range(4)], axis=0)
        total = lax.dot_general(parts, toeplitz, NT, preferred_element_type=F32)
        square = jnp.sum(total * total, axis=1, keepdims=True)
        power = sum(square[CH * m : CH * (m + 1)] for m in range(4)) / L
        scale = lax.rsqrt(power + 1e-06)
        for m in range(4):
            lanes = slice(L * w + 256 * m, L * w + 256 * (m + 1))
            white[:, lanes] = (total[CH * m : CH * (m + 1)] * scale).astype(BF16)


def gapped(block):
    zeros = jnp.zeros((block.shape[0], GAP), BF16)
    return jnp.concatenate([block[:, :L], zeros, block[:, L:], zeros], axis=1)


class Ring:
    def __init__(self, right, left, far, to_r, to_l, to_f, hop_r, hop_l, got_r, got_l, got_f, send, recv):
        self.right, self.left, self.far = right, left, far
        self.to_r, self.to_l, self.to_f, self.hop_r, self.hop_l = to_r, to_l, to_f, hop_r, hop_l
        self.got_r, self.got_l, self.got_f = got_r, got_l, got_f
        self.send, self.recv = send, recv
        self.half = to_r.shape[1] // 2 // 16 * 16

    def copy(self, c, k, merged):
        lo, hi = pl.ds(0, self.half), pl.ds(self.half, self.to_r.shape[1] - self.half)
        if merged:
            src, dst, to = (
                (self.to_f.at[c, lo], self.hop_r.at[c], self.right),
                (self.to_f.at[c, hi], self.hop_l.at[c], self.left),
                (self.to_r.at[c, hi], self.got_l.at[c, hi], self.right),
                (self.to_l.at[c, lo], self.got_r.at[c, lo], self.left),
                (self.to_r.at[c, lo], self.got_l.at[c, lo], self.right),
                (self.to_l.at[c, hi], self.got_r.at[c, hi], self.left),
            )[k]
        else:
            rows = (lo, hi)[k // 3]
            src, dst, to = (
                (self.to_f, self.got_f, self.far),
                (self.to_r, self.got_l, self.right),
                (self.to_l, self.got_r, self.left),
            )[k % 3]
            src, dst = src.at[c, rows], dst.at[c, rows]
        return pltpu.make_async_remote_copy(
            src_ref=src, dst_ref=dst, send_sem=self.send.at[c, k], recv_sem=self.recv.at[c, k],
            device_id={"day": to}, device_id_type=MESH,
        )


def reduce_kernel(
    own, middle, near, out,
    astack, bstack, distant, c_own, c_r, c_l, s_buf, z_buf, t_buf, e_own, e_send, e_got,
    x_r, x_l, x_f, x_hr, x_hl, x_gr, x_gl, x_gf, xs, xd,
    z_r, z_l, z_f, z_hr, z_hl, z_gr, z_gl, z_gf, zs, zd,
    es, ed, ps, pd,
):
    day, chan = lax.axis_index("day"), lax.axis_index("chan")
    x, zh = day // RING, day % RING
    x_to = [((x + k) % RING) * RING + zh for k in range(RING)]
    z_to = [x * RING + (zh + k) % RING for k in range(RING)]
    far_to = lax.axis_size("chan") - 1 - chan
    barrier = pltpu.get_barrier_semaphore()
    for other in (*x_to[1:], *z_to[1:]):
        pl.semaphore_signal(barrier, inc=1, device_id={"day": other}, device_id_type=MESH)
    pl.semaphore_signal(barrier, inc=1, device_id={"chan": far_to}, device_id_type=MESH)

    xring = Ring(x_to[1], x_to[3], x_to[2], x_r, x_l, x_f, x_hr, x_hl, x_gr, x_gl, x_gf, xs, xd)
    zring = Ring(z_to[1], z_to[3], z_to[2], z_r, z_l, z_f, z_hr, z_hl, z_gr, z_gl, z_gf, zs, zd)

    def block_copy(h):
        rows = pl.ds(PART * h, PART)
        return pltpu.make_async_remote_copy(
            src_ref=own.at[rows], dst_ref=distant.at[rows], send_sem=ps.at[h], recv_sem=pd.at[h],
            device_id={"chan": far_to}, device_id_type=MESH,
        )

    mine = gapped(own[...])
    for a in range(DELAYS):
        moved = pltpu.roll(mine, a, 1) if a else mine
        for part in range(RING):
            astack[part, 16 * a : 16 * a + 16, :] = moved[16 * part : 16 * part + 16]

    norm = 1.0 / jnp.sqrt(jnp.float32(16 * 2 * L))

    def product(k):
        return lax.dot_general(astack[(x + k) % RING], bstack[...], NT, preferred_element_type=F32)

    def compute(c, start=True):
        r, h = c // SPLIT, c % SPLIT
        merged, half = c in X_MERGED, xring.half
        if r == 2:
            block_copy(h).wait_recv()
        theirs = gapped((middle, near, distant)[r][PART * h : PART * (h + 1)])
        for b in range(4):
            shift = (MAXLAG - STEP * b) % ROW
            bstack[PART * b : PART * (b + 1), :] = pltpu.roll(theirs, shift, 1) if shift else theirs
        x_f[c] = product(2).astype(BF16)
        if start:
            x_start(c, (0, 1) if merged else (0,))
        piece = product(1)
        if merged:
            x_r[c, half:] = piece[half:].astype(BF16)
            c_r[c] = piece[:half]
        else:
            x_r[c] = piece.astype(BF16)
        if start:
            x_start(c, (2,) if merged else (1,))
        piece = product(3)
        if merged:
            x_l[c, :half] = piece[:half].astype(BF16)
            c_l[c] = piece[half:]
        else:
            x_l[c] = piece.astype(BF16)
        if start:
            x_start(c, (3,) if merged else (2, 3, 4, 5))
        c_own[c] = product(0)

    def x_start(c, which):
        for k in which:
            xring.copy(c, k, c in X_MERGED).start()

    def x_merge(c):
        half = xring.half
        xring.copy(c, 0, True).wait_recv()
        x_r[c, :half] = (c_r[c] + x_hr[c].astype(F32)).astype(BF16)
        xring.copy(c, 4, True).start()
        xring.copy(c, 1, True).wait_recv()
        x_l[c, half:] = (c_l[c] + x_hl[c].astype(F32)).astype(BF16)
        xring.copy(c, 5, True).start()

    def x_halves(c):
        for g in range(2):
            for k in range(3 * g, 3 * g + 3):
                xring.copy(c, k, False).wait_recv()
            rows = slice(0, xring.half) if g == 0 else slice(xring.half, XR)
            total = c_own[c, rows] + x_gl[c, rows].astype(F32) + x_gr[c, rows].astype(F32) + x_gf[c, rows].astype(F32)
            for side in range(WIDE // 128):
                lanes = slice(128 * side, 128 * (side + 1))
                s_buf[side, rows] = total[:, lanes]
                for part in range(RING):
                    for i in range(4):
                        z_buf[c, part, 32 * g + 8 * i : 32 * g + 8 * i + 8, lanes] = s_buf[
                            side, pl.ds(128 * g + 4 * part + i, 8, stride=16), :
                        ]
            half = pl.ds(32 * g, 32)
            for k, ref, off in ((0, z_f, 2), (1, z_r, 1), (2, z_l, 3)):
                ref[c, half] = z_buf[c, (zh + off) % RING, half].astype(BF16)
                zring.copy(c, 3 * g + k, False).start()
            if g:
                e_own[:, PART * c : PART * (c + 1)] = total[128:144, 3 * PART :]

    def x_end(c):
        merged = c in X_MERGED
        if not merged:
            return x_halves(c)
        for k in range(2, 6) if merged else range(3):
            xring.copy(c, k, merged).wait_recv()
        total = c_own[c] + x_gl[c].astype(F32) + x_gr[c].astype(F32)
        if not merged:
            total += x_gf[c].astype(F32)
        for side in range(WIDE // 128):
            lanes = slice(128 * side, 128 * (side + 1))
            s_buf[side] = total[:, lanes]
            for part in range(RING):
                for i in range(4):
                    z_buf[c, part, 16 * i : 16 * i + 16, lanes] = s_buf[side, pl.ds(4 * part + i, 16, stride=16), :]
        e_own[:, PART * c : PART * (c + 1)] = total[256:272, 3 * PART :]
        merged = c in Z_MERGED
        z_f[c] = z_buf[c, (zh + 2) % RING].astype(BF16)
        if not merged:
            zring.copy(c, 0, merged).start()
            z_r[c] = z_buf[c, (zh + 1) % RING].astype(BF16)
            zring.copy(c, 1, merged).start()
            z_l[c] = z_buf[c, (zh + 3) % RING].astype(BF16)
            zring.copy(c, 2, merged).start()
        else:
            zring.copy(c, 0, merged).start()
            zring.copy(c, 1, merged).start()
            half = zring.half
            z_r[c, half:] = z_buf[c, (zh + 1) % RING, half:].astype(BF16)
            zring.copy(c, 2, merged).start()
            z_l[c, :half] = z_buf[c, (zh + 3) % RING, :half].astype(BF16)
            zring.copy(c, 3, merged).start()

    def z_merge(c):
        half = zring.half
        zring.copy(c, 0, True).wait_recv()
        z_r[c, :half] = (z_buf[c, (zh + 1) % RING, :half] + z_hr[c].astype(F32)).astype(BF16)
        zring.copy(c, 4, True).start()
        zring.copy(c, 1, True).wait_recv()
        z_l[c, half:] = (z_buf[c, (zh + 3) % RING, half:] + z_hl[c].astype(F32)).astype(BF16)
        zring.copy(c, 5, True).start()

    def z_end(c):
        merged = c in Z_MERGED
        for k in range(2, 6) if merged else range(6):
            zring.copy(c, k, merged).wait_recv()
        total = z_buf[c, zh] + z_gl[c].astype(F32) + z_gr[c].astype(F32)
        if not merged:
            total += z_gf[c].astype(F32)
        if merged:
            t_buf[c] = total * norm
        else:
            for g in range(2):
                for i in range(4):
                    t_buf[c, 16 * i + 8 * g : 16 * i + 8 * g + 8] = total[32 * g + 8 * i : 32 * g + 8 * i + 8] * norm
        if c % SPLIT == SPLIT - 1:
            first = c + 1 - SPLIT
            for b in range(4):
                cut = [t_buf[first + h, :, PART * b : PART * (b + 1)] for h in range(SPLIT)]
                out[c // SPLIT, 16 * b : 16 * b + 16, :] = jnp.concatenate(
                    [cut[h][16 * i : 16 * i + 16] for i in range(4) for h in range(SPLIT)], axis=1
                )

    def e_copy(k):
        return pltpu.make_async_remote_copy(
            src_ref=e_send, dst_ref=e_got.at[k - 1], send_sem=es.at[k - 1], recv_sem=ed.at[k - 1],
            device_id={"day": z_to[k]}, device_id_type=MESH,
        )

    steps = {"C": compute, "M": x_merge, "X": x_end, "N": z_merge, "Z": z_end}
    compute(0, start=False)
    pl.semaphore_wait(barrier, 7)
    for h in range(SPLIT):
        block_copy(h).start()
    x_start(0, range(4) if 0 in X_MERGED else range(3))
    for step in ORDER:
        steps[step[0]](int(step[1:]))
        if step == LAST:
            e_send[...] = e_own[...].astype(BF16)
            for k in range(1, RING):
                e_copy(k).start()

    for k in range(1, RING):
        e_copy(k).wait_recv()
    tails = (e_own[...] + sum(e_got[k].astype(F32) for k in range(3))) * norm
    tail = tails[0:4]
    for part in range(1, RING):
        tail = jnp.where(zh == part, tails[4 * part : 4 * part + 4], tail)
    for r in range(3):
        out[r, 64:65, :] = jnp.concatenate([tail[i : i + 1, CH * r : CH * (r + 1)] for i in range(4)], axis=1)

    for k in range(1, RING):
        e_copy(k).wait_send()
    for h in range(SPLIT):
        block_copy(h).wait_send()
    for c in range(CHUNKS):
        for k in range(6):
            xring.copy(c, k, c in X_MERGED).wait_send()
        for k in range(6):
            zring.copy(c, k, c in Z_MERGED).wait_send()


def exchange_kernel(mask, own, middle, near, send, recv):
    chan, count = lax.axis_index("chan"), lax.axis_size("chan")
    flip = sum((1 - 2 * (chan // 2**k % 2)) * 2**k for k in range(count.bit_length() - 1) if mask >> k & 1)
    to = (chan + flip, chan + 1 - 2 * (chan % 2))
    barrier = pltpu.get_barrier_semaphore()
    for other in to:
        pl.semaphore_signal(barrier, inc=1, device_id={"chan": other}, device_id_type=MESH)
    pl.semaphore_wait(barrier, 2)
    copies = [
        pltpu.make_async_remote_copy(
            src_ref=own, dst_ref=dst, send_sem=send.at[k], recv_sem=recv.at[k],
            device_id={"chan": to[k]}, device_id_type=MESH,
        )
        for k, dst in enumerate((middle, near))
    ]
    for copy in copies:
        copy.start()
    for copy in copies:
        copy.wait()


def exchange(white, mask):
    vmem = pl.BlockSpec(memory_space=pltpu.VMEM)
    shape = jax.ShapeDtypeStruct(white.shape, white.dtype)
    return pl.pallas_call(
        functools.partial(exchange_kernel, mask),
        out_shape=(shape,) * 2,
        in_specs=[vmem],
        out_specs=(vmem,) * 2,
        scratch_shapes=[pltpu.SemaphoreType.DMA((2,)), pltpu.SemaphoreType.DMA((2,))],
        compiler_params=pltpu.CompilerParams(collective_id=mask, has_side_effects=True, vmem_limit_bytes=8 << 20),
        name=f"exchange{mask}",
    )(white)


def correlate(white, other, near):
    def chunks(rows, kind=BF16):
        return pltpu.VMEM((CHUNKS, rows, WIDE), kind)

    def sems(*shape):
        return pltpu.SemaphoreType.DMA(shape)

    vmem = pl.BlockSpec(memory_space=pltpu.VMEM)
    return pl.pallas_call(
        reduce_kernel,
        out_shape=jax.ShapeDtypeStruct((3, LAGS, 256), F32),
        in_specs=[vmem] * 3,
        out_specs=vmem,
        scratch_shapes=[
            pltpu.VMEM((RING, XR, ROW), BF16),
            pltpu.VMEM((WIDE, ROW), BF16),
            pltpu.VMEM((CH, 2 * L), BF16),
            chunks(XR, F32),
            chunks(XR // 32 * 16, F32),
            chunks(XR - XR // 32 * 16, F32),
            pltpu.VMEM((WIDE // 128, XR, 128), F32),
            pltpu.VMEM((CHUNKS, RING, ZR, WIDE), F32),
            chunks(ZR, F32),
            pltpu.VMEM((16, CHUNKS * PART), F32),
            pltpu.VMEM((16, CHUNKS * PART), BF16),
            pltpu.VMEM((3, 16, CHUNKS * PART), BF16),
            *[chunks(XR) for _ in range(3)],
            chunks(XR // 32 * 16),
            chunks(XR - XR // 32 * 16),
            *[chunks(XR) for _ in range(3)],
            sems(CHUNKS, 6), sems(CHUNKS, 6),
            *[chunks(ZR) for _ in range(3)],
            *[chunks(ZR // 2) for _ in range(2)],
            *[chunks(ZR) for _ in range(3)],
            sems(CHUNKS, 6), sems(CHUNKS, 6),
            sems(3), sems(3),
            sems(SPLIT), sems(SPLIT),
        ],
        compiler_params=pltpu.CompilerParams(collective_id=0, has_side_effects=True, vmem_limit_bytes=48 << 20),
        name="correlate",
    )(white, other, near)


def local(records, filter_taps, window_offsets, pair_masks):
    count = lax.axis_size("chan")
    middle = jnp.sum(pair_masks) - count
    vmem = pl.BlockSpec(memory_space=pltpu.VMEM)
    white = pl.pallas_call(
        whiten_kernel,
        out_shape=jax.ShapeDtypeStruct((CH, 2 * L), BF16),
        in_specs=[pl.BlockSpec(memory_space=pltpu.SMEM), vmem, vmem],
        out_specs=vmem,
        scratch_shapes=[pltpu.VMEM((8, 384), F32)],
        compiler_params=pltpu.CompilerParams(vmem_limit_bytes=16 << 20),
        name="whiten",
    )(window_offsets, records[0], filter_taps[None])

    branches = [functools.partial(exchange, mask=m) for m in range(2, count - 1)]
    other, near = lax.switch(middle - 2, branches, white)
    res = correlate(white, other, near)
    kind = pair_masks[:, None, None]
    return jnp.where(kind == 1, res[1], jnp.where(kind == count - 1, res[2], res[0]))


def solution(mesh):
    in_specs = (P("day", "chan", None), P(), P("day", None), P())
    out_specs = P(None, None, ("chan", "day"))
    return jax.shard_map(local, mesh=mesh, in_specs=in_specs, out_specs=out_specs, check_vma=False)
```
